32 devices in a mesh: grp: 16 (over z, x, core), blk: 2 (over y).
Axes of the slice: x: 2, y: 2, z: 4, core: 2. Of those that a mesh axis runs over, the one named last changes fastest.
Arguments:
- walker_matrix: float32 [16, 2, 1024, 1024], P('grp', 'blk'), may hold values from -6 to 6
- updates: bfloat16 [16, 2, 4, 1024, 256], P('grp', 'blk'), may hold values from -0.19921875 to 0.19921875
- update_rows: int32 [16, 2, 4, 256], P('grp', 'blk'), may hold values from 0 to 1023, as said below
- left_table: float32 [1024, 256], replicated, may hold values from -0.1875 to 0.1875
- right_table: float32 [1024, 256], replicated, may hold values from -0.1875 to 0.1875
- assignment: int32 [2, 16], P('blk'), may hold values from 0 to 15, each once within a row
- momentum_sum: int32 [16, 16], replicated, may hold values from 0 to 15, as said below
- transfer_momentum: int32 [8], replicated, may hold values from 0 to 15
- transfer_frequency: int32 [8], replicated, may hold values from 0 to 15
- ownership: int32 [8], P('blk'), may hold values from 0 to 7, each once
- g4_prior: float32 [16, 8, 256, 256], P('grp', 'blk'), may hold values from -6 to 6
Outputs:
- g4_slices: float32 [16, 8, 256, 256], P('grp', 'blk')
The draws below stay inside these ranges and needn't reach their ends.
Inputs may be any that keep to these rules, and one draw needn't show every extreme that they name: `update_rows`: within each update of each walker the 256 row indices are distinct. `assignment`: each row is a permutation of the grp indices. `momentum_sum`: the addition table of a periodic 4 x 4 cluster under a relabeling of its momenta; every row and column is a permutation. `ownership`: a permutation of the transfer slots.
All inputs are finite; a program needn't handle non-finite values.
Results may differ from the reference program's by a relative error of at most 0.0003.
Values sent between devices are 32-bit elements; how exact they have to be, the bound alone decides.
A program may use at most 128 MiB of HBM per device.

```python
import jax
import jax.numpy as jnp
from jax import lax

ORDER = 1024
RANK = 256
UPD = 4
CL = 4
NW = 16
NK = 16
KW = 256
Q = 8
N_GRP = 16
N_BLK = 2


def draw_update_rows(key, part):
    keys = jax.random.split(jax.random.fold_in(key, 11), N_GRP * N_BLK * UPD)
    drawn = jax.vmap(lambda one_key: jax.random.permutation(one_key, ORDER)[:RANK])(keys)
    return drawn.reshape(N_GRP, N_BLK, UPD, RANK).astype(jnp.int32)


def draw_momentum_sum(key, part):
    relabel = jax.random.permutation(jax.random.fold_in(key, 17), NK).astype(jnp.int32)
    inverse = jnp.zeros((NK,), jnp.int32).at[relabel].set(jnp.arange(NK, dtype=jnp.int32))
    first = inverse[:, None]
    second = inverse[None, :]
    combined = (first // CL + second // CL) % CL * CL + (first % CL + second % CL) % CL
    return relabel[combined].astype(jnp.int32)


def with_ends(values, own_key, least, largest):
    longest = values.shape.index(max(values.shape))
    spots = []
    for shift in (0, 1):
        where = [jax.random.randint(jax.random.fold_in(own_key, axis), (), 0, length) for axis, length in enumerate(values.shape)]
        where[longest] = (where[longest] + shift) % values.shape[longest]
        spots.append(tuple(where))
    return values.at[spots[0]].set(least).at[spots[1]].set(largest)


def level_of(rng, dims, shards, smallest, largest):
    def one(dim, shards_of):
        heights = jax.random.uniform(jax.random.fold_in(jax.random.fold_in(rng, 6), dim), (shards_of,), jnp.float32, smallest / len(shards), largest / len(shards))
        return jnp.repeat(jnp.exp(heights), dims[dim] // shards_of).reshape((-1,) + (1,) * (len(dims) - dim - 1))

    loudness = one(*shards[0])
    for cut in shards[1:]:
        loudness = loudness * one(*cut)
    return loudness


def noise(key, dims, scale, bound, cuts=(), kind=jnp.bfloat16):
    loudness = level_of(key, dims, cuts, -0.22, 0.18) if cuts else 1.0
    entries = jax.random.normal(key, dims, jnp.float32) * scale * loudness
    return jnp.minimum(jnp.maximum(entries, -bound), bound).astype(kind)


def setup_inputs(seed: int = 0) -> dict:
    arg_keys = jax.random.split(jax.random.key(seed), 12)
    return {
        "walker_matrix": noise(arg_keys[0], (N_GRP, N_BLK, ORDER, ORDER), 1.0, 6.0, ((0, 16), (1, 2)), jnp.float32),
        "updates": noise(arg_keys[1], (N_GRP, N_BLK, UPD, ORDER, RANK), 0.03125, 0.19921875, ((0, 16), (1, 2))),
        "update_rows": draw_update_rows(jax.random.fold_in(arg_keys[11], 71), 0),
        "left_table": noise(arg_keys[3], (ORDER, KW), ORDER ** -0.5, 0.1875, (), jnp.float32),
        "right_table": noise(arg_keys[4], (ORDER, KW), ORDER ** -0.5, 0.1875, (), jnp.float32),
        "assignment": jax.vmap(lambda own: jax.random.permutation(own, N_GRP))(jax.random.split(arg_keys[5], N_BLK)).reshape((N_BLK, N_GRP)).astype(jnp.int32),
        "momentum_sum": draw_momentum_sum(jax.random.fold_in(arg_keys[11], 71), 0),
        "transfer_momentum": with_ends(jax.random.randint(arg_keys[7], (Q,), 0, NK), jax.random.fold_in(arg_keys[7], 1), 0, NK - 1).astype(jnp.int32),
        "transfer_frequency": with_ends(jax.random.randint(arg_keys[8], (Q,), 0, NW), jax.random.fold_in(arg_keys[8], 1), 0, NW - 1).astype(jnp.int32),
        "ownership": jax.random.permutation(arg_keys[9], Q).astype(jnp.int32),
        "g4_prior": noise(arg_keys[10], (N_GRP, Q, KW, KW), 1.0, 6.0, ((0, 16), (1, 2)), jnp.float32),
    }


highest = lax.Precision.HIGHEST


def measure_walker(matrix, updates_here, rows_here, left_table, right_table):
    for number in range(UPD):
        picked = matrix[rows_here[number]]
        matrix = matrix + jnp.dot(updates_here[number].astype(jnp.float32), picked, precision=highest)
    partial_value = jnp.dot(matrix, right_table, precision=highest)
    return jnp.dot(left_table.T, partial_value, precision=highest)


def shift_rows(momentum_sum, moment_ids, freq_ids):
    labels = jnp.arange(KW, dtype=jnp.int32)
    momenta = labels // NW
    frequency = labels % NW
    return momentum_sum[momenta[None, :], moment_ids[:, None]] * NW + (frequency[None, :] + freq_ids[:, None]) % NW


def cycle_terms(greens_cycle, shifted):
    flipped = jnp.swapaxes(greens_cycle, 1, 2)

    def one_transfer(row_ids):
        picked = jnp.take(flipped, row_ids, axis=1)
        picked = jnp.take(picked, row_ids, axis=2)
        return jnp.sum(greens_cycle * picked, axis=0)

    return jax.vmap(one_transfer)(shifted)


def reference(walker_matrix, updates, update_rows, left_table, right_table, assignment, momentum_sum, transfer_momentum, transfer_frequency, ownership, g4_prior):
    walkers = N_GRP * N_BLK
    greens = lax.map(lambda walker_items: measure_walker(walker_items[0], walker_items[1], walker_items[2], left_table, right_table),
                     (walker_matrix.reshape(walkers, ORDER, ORDER), updates.reshape(walkers, UPD, ORDER, RANK), update_rows.reshape(walkers, UPD, RANK)))
    greens = greens.reshape(N_GRP, N_BLK, KW, KW)
    chosen = (assignment[:, :, None] == jnp.arange(N_GRP, dtype=jnp.int32)[None, None, :]).astype(jnp.float32)
    measured = jnp.einsum("bwa,wbij->abij", chosen, greens, precision=highest)
    shifted = shift_rows(momentum_sum, transfer_momentum[ownership], transfer_frequency[ownership])
    summed = lax.map(lambda cycle_greens: cycle_terms(cycle_greens, shifted), measured)
    return g4_prior + summed * (1.0 / N_BLK)
```

```python
import functools

import jax
import jax.numpy as jnp
from jax import lax
from jax.experimental import pallas as pl
from jax.experimental.pallas import tpu as pltpu
from jax.sharding import PartitionSpec as P

MESH = pl.DeviceIdType.MESH
F32 = jnp.float32
BF16 = jnp.bfloat16


def split(x):
    hi = x.astype(BF16)
    return hi, (x - hi.astype(F32)).astype(BF16)


def nn(a, b):
    return jnp.dot(a, b, preferred_element_type=F32)


def nt(a, b):
    return lax.dot_general(a, b, (((1,), (1,)), ((), ())), preferred_element_type=F32)


def walker_kernel(m_hbm, u_hbm, rows_ref, l_hbm, r_hbm, out_ref, m_v, u_v, l_v, r_v, sems):
    number, order, rank = u_v.shape
    parts = 4
    step = order // parts
    copy_l = pltpu.make_async_copy(l_hbm, l_v, sems.at[0])
    copy_r = pltpu.make_async_copy(r_hbm, r_v, sems.at[1])
    copy_u = [pltpu.make_async_copy(u_hbm.at[i], u_v.at[i], sems.at[2 + i]) for i in range(number)]
    copy_m = [
        pltpu.make_async_copy(m_hbm.at[pl.ds(i * step, step)], m_v.at[pl.ds(i * step, step)], sems.at[2 + number + i])
        for i in range(parts)
    ]
    copy_l.start()
    for i in reversed(range(number)):
        copy_u[i].start()
    for c in copy_m:
        c.start()
    copy_r.start()
    copy_l.wait()
    w = jnp.transpose(l_v[...])
    for i in reversed(range(number)):
        pick = jnp.where(
            lax.broadcasted_iota(jnp.int32, (order, rank), 0) == rows_ref[pl.ds(i, 1), :], 1.0, 0.0
        ).astype(BF16)
        hi, lo = split(w)
        copy_u[i].wait()
        u = u_v[i]
        thi, tlo = split(nn(hi, u) + nn(lo, u))
        w = w + (nt(thi, pick) + nt(tlo, pick))
    hi, lo = split(w)
    v = None
    for i in range(parts):
        copy_m[i].wait()
        mh, ml = split(m_v[pl.ds(i * step, step), :])
        a, b = hi[:, i * step:(i + 1) * step], lo[:, i * step:(i + 1) * step]
        term = nn(a, mh) + nn(a, ml) + nn(b, mh)
        v = term if v is None else v + term
    vh, vl = split(v)
    copy_r.wait()
    rh, rl = split(r_v[...])
    out_ref[...] = nn(vh, rh) + nn(vh, rl) + nn(vl, rh)


def exchange_kernel(groups, blocks, target_ref, g_ref, out_ref, spread, arranged, s1, r1, s2, r2, s3, r3):
    grp = lax.axis_index("grp")
    blk = lax.axis_index("blk")

    def group_peer(i):
        return {"grp": lax.rem(grp + i, groups), "blk": blk}

    def block_peer(i):
        return {"grp": grp, "blk": lax.rem(blk + i, blocks)}

    barrier = pltpu.get_barrier_semaphore()

    @pl.loop(1, groups)
    def _(i):
        pl.semaphore_signal(barrier, inc=1, device_id=group_peer(i), device_id_type=MESH)

    @pl.loop(1, blocks)
    def _(i):
        pl.semaphore_signal(barrier, inc=1, device_id=block_peer(i), device_id_type=MESH)

    pl.semaphore_wait(barrier, groups + blocks - 2)

    def first(i):
        return pltpu.make_async_remote_copy(
            g_ref.at[lax.rem(grp + i, groups)], spread.at[grp], s1.at[i], r1.at[i],
            device_id=group_peer(i), device_id_type=MESH)

    def second(i):
        return pltpu.make_async_remote_copy(
            arranged.at[lax.rem(grp + i, groups)], out_ref.at[blk, grp], s2.at[i], r2.at[i],
            device_id=group_peer(i), device_id_type=MESH)

    def third(i, k):
        piece = out_ref.at[blk, lax.rem(grp + groups - i, groups)]
        return pltpu.make_async_remote_copy(
            piece, piece, s3.at[i, k], r3.at[i, k], device_id=block_peer(k), device_id_type=MESH)

    @pl.loop(1, groups)
    def _(i):
        first(i).start()

    spread[grp] = g_ref[grp]

    def source_of(a):
        return lax.fori_loop(0, groups, lambda w, s: jnp.where(target_ref[0, w] == a, w, s), 0)

    @pl.loop(1, groups)
    def _(i):
        first(i).wait_recv()

    @pl.loop(1, groups)
    def _(i):
        a = lax.rem(grp + i, groups)
        arranged[a] = spread[source_of(a)]
        second(i).start()

    out_ref[blk, grp] = spread[source_of(grp)]

    for k in range(1, blocks):
        third(0, k).start()

    @pl.loop(1, groups)
    def _(i):
        second(i).wait_recv()
        for k in range(1, blocks):
            third(i, k).start()

    @pl.loop(0, groups)
    def _(i):
        for k in range(1, blocks):
            third(i, k).wait_recv()

    @pl.loop(0, groups)
    def _(i):
        for k in range(1, blocks):
            third(i, k).wait_send()

    @pl.loop(1, groups)
    def _(i):
        first(i).wait_send()
        second(i).wait_send()


def cycle_kernel(own_ref, mom_ref, freq_ref, sum_ref, g_ref, prior_ref, out_ref, parts_v, perm_v):
    j = pl.program_id(0)
    blocks, kw, _ = g_ref.shape
    momenta = sum_ref.shape[0]
    nw = kw // momenta

    @pl.when(j == 0)
    def _():
        for b in range(blocks):
            hi, lo = split(g_ref[b])
            parts_v[b, :kw, :] = hi
            parts_v[b, kw:, :] = lo

    t = own_ref[j]
    q = mom_ref[t]
    f = freq_ref[t]
    lane = lax.broadcasted_iota(jnp.int32, (nw, kw), 1)
    nu = lax.rem(lax.broadcasted_iota(jnp.int32, (nw, kw), 0) + f, nw)
    base = lane - nu
    for kappa in range(momenta):
        hit = jnp.where(base == sum_ref[kappa, q] * nw, 1.0, 0.0).astype(BF16)
        perm_v[kappa * nw:(kappa + 1) * nw, :kw] = hit
        perm_v[kappa * nw:(kappa + 1) * nw, kw:] = hit
    both = perm_v[...]
    total = None
    for b in range(blocks):
        x = nt(both[:, :kw], parts_v[b]).astype(BF16)
        term = g_ref[b] * nt(x, both)
        total = term if total is None else total + term
    out_ref[0] = prior_ref[0] + total * (1.0 / blocks)


def shards(
    walker_matrix,
    updates,
    update_rows,
    left_table,
    right_table,
    assignment,
    momentum_sum,
    transfer_momentum,
    transfer_frequency,
    ownership,
    g4_prior,
):
    groups = lax.axis_size("grp")
    blocks = lax.axis_size("blk")
    order, kw = left_table.shape
    number, rank = updates.shape[2], updates.shape[4]
    anyspace = pl.BlockSpec(memory_space=pl.ANY)
    vmem = pl.BlockSpec(memory_space=pltpu.VMEM)
    smem = pl.BlockSpec(memory_space=pltpu.SMEM)
    greens = pl.pallas_call(
        walker_kernel,
        out_shape=jax.ShapeDtypeStruct((kw, kw), F32),
        in_specs=[anyspace, anyspace, vmem, anyspace, anyspace],
        out_specs=vmem,
        scratch_shapes=[
            pltpu.VMEM((order, order), F32),
            pltpu.VMEM((number, order, rank), BF16),
            pltpu.VMEM((order, kw), F32),
            pltpu.VMEM((order, kw), F32),
            pltpu.SemaphoreType.DMA((number + 6,)),
        ],
        compiler_params=pltpu.CompilerParams(vmem_limit_bytes=48 * 2**20),
        name="walker",
    )(walker_matrix[0, 0], updates[0, 0], update_rows[0, 0], left_table, right_table)

    rows = kw // groups
    measured = pl.pallas_call(
        functools.partial(exchange_kernel, groups, blocks),
        out_shape=jax.ShapeDtypeStruct((blocks, groups, rows, kw), F32),
        in_specs=[smem, vmem],
        out_specs=vmem,
        scratch_shapes=[
            pltpu.VMEM((groups, rows, kw), F32),
            pltpu.VMEM((groups, rows, kw), F32),
            pltpu.SemaphoreType.DMA((groups,)),
            pltpu.SemaphoreType.DMA((groups,)),
            pltpu.SemaphoreType.DMA((groups,)),
            pltpu.SemaphoreType.DMA((groups,)),
            pltpu.SemaphoreType.DMA((groups, blocks)),
            pltpu.SemaphoreType.DMA((groups, blocks)),
        ],
        compiler_params=pltpu.CompilerParams(
            collective_id=0, has_side_effects=True, vmem_limit_bytes=16 * 2**20),
        name="exchange",
    )(assignment, greens.reshape(groups, rows, kw)).reshape(blocks, kw, kw)

    slots = g4_prior.shape[1]
    whole = pl.BlockSpec((blocks, kw, kw), lambda j, *_: (0, 0, 0))
    block = pl.BlockSpec((1, kw, kw), lambda j, *_: (j, 0, 0))
    out = pl.pallas_call(
        cycle_kernel,
        out_shape=jax.ShapeDtypeStruct((slots, kw, kw), F32),
        grid_spec=pltpu.PrefetchScalarGridSpec(
            num_scalar_prefetch=4,
            grid=(slots,),
            in_specs=[whole, block],
            out_specs=block,
            scratch_shapes=[
                pltpu.VMEM((blocks, 2 * kw, kw), BF16),
                pltpu.VMEM((kw, 2 * kw), BF16),
            ],
        ),
        compiler_params=pltpu.CompilerParams(vmem_limit_bytes=24 * 2**20),
        name="cycle",
    )(ownership, transfer_momentum, transfer_frequency, momentum_sum, measured, g4_prior[0])
    return out[None]


def solution(mesh):
    placed = (
        P("grp", "blk", None, None),
        P("grp", "blk", None, None, None),
        P("grp", "blk", None, None),
        P(),
        P(),
        P("blk", None),
        P(),
        P(),
        P(),
        P("blk"),
        P("grp", "blk", None, None),
    )
    return jax.shard_map(
        shards, mesh=mesh, in_specs=placed, out_specs=P("grp", "blk", None, None), check_vma=False
    )
```

```python
import functools

import jax
import jax.numpy as jnp
from jax import lax
from jax.experimental import pallas as pl
from jax.experimental.pallas import tpu as pltpu
from jax.sharding import PartitionSpec as P

MESH = pl.DeviceIdType.MESH
F32 = jnp.float32
BF16 = jnp.bfloat16


def split(x):
    hi = x.astype(BF16)
    return hi, (x - hi.astype(F32)).astype(BF16)


def nn(a, b):
    return jnp.dot(a, b, preferred_element_type=F32)


def nt(a, b):
    return lax.dot_general(a, b, (((1,), (1,)), ((), ())), preferred_element_type=F32)


def exchange_kernel(
    groups, blocks, target_ref, own_ref, mom_ref, freq_ref, sum_ref, m_hbm, u_hbm, rows_hbm, l_hbm, r_hbm, out_hbm,
    m_v, u_v, rows_v, l_v, r_v, pick_v, zh_v, zl_v, g_v, arranged, out_ref, perm_v, total_v, source,
    sems, out_sems, s1, r1, s2, r2, s3, r3, *spread,
):
    grp = lax.axis_index("grp")
    blk = lax.axis_index("blk")
    number, order, rank = u_v.shape
    halves, _, rows, kw = g_v.shape
    kh = kw // halves
    parts = 4
    step = order // parts

    def group_peer(i):
        return {"grp": lax.rem(grp + i, groups), "blk": blk}

    def block_peer(i):
        return {"grp": grp, "blk": lax.rem(blk + i, blocks)}

    copy_rows = pltpu.make_async_copy(rows_hbm, rows_v, sems.at[0])
    copy_l = pltpu.make_async_copy(l_hbm, l_v, sems.at[1])
    copy_r = pltpu.make_async_copy(r_hbm, r_v, sems.at[2])
    copy_u = [pltpu.make_async_copy(u_hbm.at[i], u_v.at[i], sems.at[3 + i]) for i in range(number)]
    copy_m = [
        pltpu.make_async_copy(m_hbm.at[pl.ds(i * step, step)], m_v.at[pl.ds(i * step, step)], sems.at[3 + number + i])
        for i in range(parts)
    ]
    copy_rows.start()
    copy_l.start()
    for i in reversed(range(number)):
        copy_u[i].start()
    copy_r.start()
    for c in copy_m:
        c.start()

    barrier = pltpu.get_barrier_semaphore()

    @pl.loop(1, groups)
    def _(i):
        pl.semaphore_signal(barrier, inc=1, device_id=group_peer(i), device_id_type=MESH)

    @pl.loop(1, blocks)
    def _(i):
        pl.semaphore_signal(barrier, inc=1, device_id=block_peer(i), device_id_type=MESH)

    targets = [target_ref[0, w] for w in range(groups)]
    for a in range(groups):
        found = 0
        for w in range(groups):
            found = jnp.where(targets[w] == a, w, found)
        source[a] = found

    copy_rows.wait()
    for i in reversed(range(number)):
        pick_v[i] = jnp.where(
            lax.broadcasted_iota(jnp.int32, (order, rank), 0) == rows_v[pl.ds(i, 1), :], 1.0, 0.0
        ).astype(BF16)

    slots = total_v.shape[0]
    momenta = sum_ref.shape[0]
    nw = kw // momenta
    sub = lax.broadcasted_iota(jnp.int32, (nw, kw), 0)
    lane = lax.broadcasted_iota(jnp.int32, (nw, kw), 1)
    for j in range(slots):
        t = own_ref[j]
        q = mom_ref[t]
        moved = sub + freq_ref[t]
        base = lane - jnp.where(moved >= nw, moved - nw, moved)
        for kappa in range(momenta):
            hit = jnp.where(base == sum_ref[kappa, q] * nw, 1.0, 0.0).astype(BF16)
            perm_v[j * kw + kappa * nw:j * kw + (kappa + 1) * nw, :] = hit

    def accumulate(b, fresh, last):
        g = out_ref[b].reshape(kw, kw)
        gh, gl = split(g)
        xh = nt(perm_v[...], gh).astype(BF16)
        xl = nt(perm_v[...], gl).astype(BF16)
        for j in range(slots):
            rows_j = slice(j * kw, (j + 1) * kw)
            y = nt(jnp.concatenate([xh[rows_j], xl[rows_j]], axis=0), perm_v[rows_j, :])
            term = g * (y[:kw] + y[kw:])
            total_v[j] = term if fresh else total_v[j] + term
            if last:
                pltpu.make_async_copy(total_v.at[j], out_hbm.at[j], out_sems.at[j]).start()

    def chain(h):
        w = jnp.transpose(l_v[:, h * kh:(h + 1) * kh])
        for i in reversed(range(number)):
            if h == 0:
                copy_u[i].wait()
            t = nn(jnp.concatenate(split(w), axis=0), u_v[i])
            t = nt(jnp.concatenate(split(t[:kh] + t[kh:]), axis=0), pick_v[i])
            w = w + (t[:kh] + t[kh:])
        return split(w)

    def finish(h, wh, wl):
        t = nn(jnp.concatenate([wh, wl], axis=0), zh_v[...])
        g = t[:kh] + t[kh:] + nn(wh, zl_v[...])
        g_v[h] = g.reshape(groups, rows, kw)

    def first(h, i):
        return pltpu.make_async_remote_copy(
            g_v.at[h, lax.rem(grp + i, groups)], spread[h].at[grp], s1.at[h, i], r1.at[h, i],
            device_id=group_peer(i), device_id_type=MESH)

    def second(h, i):
        return pltpu.make_async_remote_copy(
            arranged.at[h, lax.rem(grp + i, groups)], out_ref.at[blk, h, grp], s2.at[h, i], r2.at[h, i],
            device_id=group_peer(i), device_id_type=MESH)

    def third(h, i, k):
        piece = out_ref.at[blk, h, lax.rem(grp + groups - i, groups)]
        return pltpu.make_async_remote_copy(
            piece, piece, s3.at[h, i, k], r3.at[h, i, k], device_id=block_peer(k), device_id_type=MESH)

    copy_l.wait()
    wh, wl = chain(0)
    copy_r.wait()
    rh, rl = split(r_v[...])
    for i in range(parts):
        copy_m[i].wait()
        mh, ml = split(m_v[pl.ds(i * step, step), :])
        t = nn(jnp.concatenate([mh, ml], axis=0), rh)
        zh, zl = split(t[:step] + t[step:] + nn(mh, rl))
        zh_v[pl.ds(i * step, step), :] = zh
        zl_v[pl.ds(i * step, step), :] = zl
    finish(0, wh, wl)

    pl.semaphore_wait(barrier, groups + blocks - 2)

    for h in range(halves):
        if h > 0:
            finish(h, *chain(h))

        @pl.loop(1, groups)
        def _(i):
            first(h, i).start()

        spread[h][grp] = g_v[h, grp]

    for h in range(halves):
        @pl.loop(1, groups)
        def _(i):
            first(h, i).wait_recv()

        @pl.loop(1, groups)
        def _(i):
            a = lax.rem(grp + i, groups)
            arranged[h, a] = spread[h][source[a]]
            second(h, i).start()

        out_ref[blk, h, grp] = spread[h][source[grp]]
        for k in range(1, blocks):
            third(h, 0, k).start()

    for h in range(halves):
        @pl.loop(1, groups)
        def _(i):
            second(h, i).wait_recv()
            for k in range(1, blocks):
                third(h, i, k).start()

    accumulate(blk, True, blocks == 1)

    for k in range(1, blocks):
        for h in range(halves):
            @pl.loop(0, groups)
            def _(i):
                third(h, i, k).wait_recv()

        accumulate(lax.rem(blk + blocks - k, blocks), False, k == blocks - 1)

    for h in range(halves):
        @pl.loop(0, groups)
        def _(i):
            for k in range(1, blocks):
                third(h, i, k).wait_send()

        @pl.loop(1, groups)
        def _(i):
            first(h, i).wait_send()
            second(h, i).wait_send()

    for j in range(slots):
        pltpu.make_async_copy(total_v.at[j], out_hbm.at[j], out_sems.at[j]).wait()


def shards(
    walker_matrix,
    updates,
    update_rows,
    left_table,
    right_table,
    assignment,
    momentum_sum,
    transfer_momentum,
    transfer_frequency,
    ownership,
    g4_prior,
):
    groups = lax.axis_size("grp")
    blocks = lax.axis_size("blk")
    order, kw = left_table.shape
    number, rank = updates.shape[2], updates.shape[4]
    smem = pl.BlockSpec(memory_space=pltpu.SMEM)
    hbm = pl.BlockSpec(memory_space=pltpu.HBM)
    halves = 2 if kw // groups % 16 == 0 else 1
    rows = kw // groups // halves
    slots = g4_prior.shape[1]
    summed = pl.pallas_call(
        functools.partial(exchange_kernel, groups, blocks),
        out_shape=jax.ShapeDtypeStruct((slots, kw, kw), F32),
        in_specs=[smem] * 5 + [hbm] * 5,
        out_specs=hbm,
        scratch_shapes=[
            pltpu.VMEM((order, order), F32),
            pltpu.VMEM((number, order, rank), BF16),
            pltpu.VMEM((number, rank), jnp.int32),
            pltpu.VMEM((order, kw), F32),
            pltpu.VMEM((order, kw), F32),
            pltpu.VMEM((number, order, rank), BF16),
            pltpu.VMEM((order, kw), BF16),
            pltpu.VMEM((order, kw), BF16),
            pltpu.VMEM((halves, groups, rows, kw), F32),
            pltpu.VMEM((halves, groups, rows, kw), F32),
            pltpu.VMEM((blocks, halves, groups, rows, kw), F32),
            pltpu.VMEM((slots * kw, kw), BF16),
            pltpu.VMEM((slots, kw, kw), F32),
            pltpu.SMEM((groups,), jnp.int32),
            pltpu.SemaphoreType.DMA((number + 7,)),
            pltpu.SemaphoreType.DMA((slots,)),
            pltpu.SemaphoreType.DMA((halves, groups)),
            pltpu.SemaphoreType.DMA((halves, groups)),
            pltpu.SemaphoreType.DMA((halves, groups)),
            pltpu.SemaphoreType.DMA((halves, groups)),
            pltpu.SemaphoreType.DMA((halves, groups, blocks)),
            pltpu.SemaphoreType.DMA((halves, groups, blocks)),
        ] + [pltpu.VMEM((groups, rows, kw), F32)] * halves,
        compiler_params=pltpu.CompilerParams(
            collective_id=0, has_side_effects=True, vmem_limit_bytes=63 * 2**20 + 2**19),
        name="exchange",
    )(assignment, ownership, transfer_momentum, transfer_frequency, momentum_sum,
      walker_matrix[0, 0], updates[0, 0], update_rows[0, 0], left_table, right_table)
    return (g4_prior[0] + summed * (1.0 / blocks))[None]


def solution(mesh):
    placed = (
        P("grp", "blk", None, None),
        P("grp", "blk", None, None, None),
        P("grp", "blk", None, None),
        P(),
        P(),
        P("blk", None),
        P(),
        P(),
        P(),
        P("blk"),
        P("grp", "blk", None, None),
    )
    return jax.shard_map(
        shards, mesh=mesh, in_specs=placed, out_specs=P("grp", "blk", None, None), check_vma=False
    )
```

```python
import functools

import jax
import jax.numpy as jnp
from jax import lax
from jax.experimental import pallas as pl
from jax.experimental.pallas import tpu as pltpu
from jax.sharding import PartitionSpec as P

MESH = pl.DeviceIdType.MESH
F32 = jnp.float32
BF16 = jnp.bfloat16


def split(x):
    hi = x.astype(BF16)
    return hi, (x - hi.astype(F32)).astype(BF16)


def nn(a, b):
    return jnp.dot(a, b, preferred_element_type=F32)


def nt(a, b):
    return lax.dot_general(a, b, (((1,), (1,)), ((), ())), preferred_element_type=F32)


def partner_order(groups):
    return list(range(1, groups))


def exchange_kernel(
    groups, blocks, target_ref, own_ref, mom_ref, freq_ref, sum_ref, m_hbm, u_hbm, rows_hbm, l_hbm, r_hbm, prior_hbm, out_hbm,
    m_v, u_v, rows_v, l_v, r_v, pick_v, zh_v, zl_v, g_v, arranged, out_ref, perm_v, total_v, source,
    sems, out_sems, s1, r1, s2, r2, s3, r3, *spread,
):
    grp = lax.axis_index("grp")
    blk = lax.axis_index("blk")
    number, order, rank = u_v.shape
    halves, _, rows, kw = g_v.shape
    kh = kw // halves
    parts = 4
    step = order // parts

    pairs = partner_order(groups)

    def partner(i):
        place, bit = grp, 1
        while bit <= i:
            if i & bit:
                place = place + bit - 2 * bit * lax.rem(grp // bit, 2)
            bit *= 2
        return place

    def group_peer(i):
        return {"grp": partner(i), "blk": blk}

    def block_peer(i):
        return {"grp": grp, "blk": lax.rem(blk + i, blocks)}

    copy_rows = pltpu.make_async_copy(rows_hbm, rows_v, sems.at[0])
    copy_l = pltpu.make_async_copy(l_hbm, l_v, sems.at[1])
    copy_r = pltpu.make_async_copy(r_hbm, r_v, sems.at[2])
    copy_u = [pltpu.make_async_copy(u_hbm.at[i], u_v.at[i], sems.at[3 + i]) for i in range(number)]
    copy_m = [
        pltpu.make_async_copy(m_hbm.at[pl.ds(i * step, step)], m_v.at[pl.ds(i * step, step)], sems.at[3 + number + i])
        for i in range(parts)
    ]
    copy_rows.start()
    copy_l.start()
    for i in reversed(range(number)):
        copy_u[i].start()
    copy_r.start()
    for c in copy_m:
        c.start()
    copy_p = pltpu.make_async_copy(prior_hbm, total_v, sems.at[3 + number + parts])
    copy_p.start()

    barrier = pltpu.get_barrier_semaphore()

    for i in pairs:
        pl.semaphore_signal(barrier, inc=1, device_id=group_peer(i), device_id_type=MESH)

    @pl.loop(1, blocks)
    def _(i):
        pl.semaphore_signal(barrier, inc=1, device_id=block_peer(i), device_id_type=MESH)

    targets = [target_ref[0, w] for w in range(groups)]
    for a in range(groups):
        found = 0
        for w in range(groups):
            found = jnp.where(targets[w] == a, w, found)
        source[a] = found

    copy_rows.wait()
    for i in reversed(range(number)):
        pick_v[i] = jnp.where(
            lax.broadcasted_iota(jnp.int32, (order, rank), 0) == rows_v[pl.ds(i, 1), :], 1.0, 0.0
        ).astype(BF16)

    slots = total_v.shape[0]
    momenta = sum_ref.shape[0]
    nw = kw // momenta
    sub = lax.broadcasted_iota(jnp.int32, (nw, kw), 0)
    lane = lax.broadcasted_iota(jnp.int32, (nw, kw), 1)
    for j in range(slots):
        t = own_ref[j]
        q = mom_ref[t]
        moved = sub + freq_ref[t]
        base = lane - jnp.where(moved >= nw, moved - nw, moved)
        for kappa in range(momenta):
            hit = jnp.where(base == sum_ref[kappa, q] * nw, 1.0, 0.0).astype(BF16)
            perm_v[j * kw + kappa * nw:j * kw + (kappa + 1) * nw, :] = hit

    def accumulate(b, last):
        g = out_ref[b].reshape(kw, kw)
        gh, gl = split(g)
        xh = nt(perm_v[...], gh).astype(BF16)
        xl = nt(perm_v[...], gl).astype(BF16)
        for j in range(slots):
            rows_j = slice(j * kw, (j + 1) * kw)
            y = nt(jnp.concatenate([xh[rows_j], xl[rows_j]], axis=0), perm_v[rows_j, :])
            term = g * (y[:kw] + y[kw:])
            term = term * (1.0 / blocks)
            total_v[j] = total_v[j] + term
            if last:
                pltpu.make_async_copy(total_v.at[j], out_hbm.at[j], out_sems.at[j]).start()

    def chain(h):
        w = jnp.transpose(l_v[:, h * kh:(h + 1) * kh])
        for i in reversed(range(number)):
            if h == 0:
                copy_u[i].wait()
            t = nn(jnp.concatenate(split(w), axis=0), u_v[i])
            t = nt(jnp.concatenate(split(t[:kh] + t[kh:]), axis=0), pick_v[i])
            w = w + (t[:kh] + t[kh:])
        return split(w)

    def finish(h, wh, wl):
        t = nn(jnp.concatenate([wh, wl], axis=0), zh_v[...])
        g = t[:kh] + t[kh:] + nn(wh, zl_v[...])
        g_v[h] = g.reshape(groups, rows, kw)

    def first(h, i):
        return pltpu.make_async_remote_copy(
            g_v.at[h, partner(i)], spread[h].at[grp], s1.at[h, i], r1.at[h, i],
            device_id=group_peer(i), device_id_type=MESH)

    def second(h, i):
        return pltpu.make_async_remote_copy(
            arranged.at[h, partner(i)], out_ref.at[blk, h, grp], s2.at[h, i], r2.at[h, i],
            device_id=group_peer(i), device_id_type=MESH)

    def third(h, i, k):
        piece = out_ref.at[blk, h, partner(i)]
        return pltpu.make_async_remote_copy(
            piece, piece, s3.at[h, i, k], r3.at[h, i, k], device_id=block_peer(k), device_id_type=MESH)

    copy_l.wait()
    wh, wl = chain(0)
    copy_r.wait()
    rh, rl = split(r_v[...])
    for i in range(parts):
        copy_m[i].wait()
        mh, ml = split(m_v[pl.ds(i * step, step), :])
        t = nn(jnp.concatenate([mh, ml], axis=0), rh)
        zh, zl = split(t[:step] + t[step:] + nn(mh, rl))
        zh_v[pl.ds(i * step, step), :] = zh
        zl_v[pl.ds(i * step, step), :] = zl
    finish(0, wh, wl)

    pl.semaphore_wait(barrier, groups + blocks - 2)

    for h in range(halves):
        if h > 0:
            finish(h, *chain(h))

        for i in pairs:
            first(h, i).start()

        spread[h][grp] = g_v[h, grp]

    def forward(h, i):
        if i:
            second(h, i).wait_recv()
        for k in range(1, blocks):
            third(h, i, k).start()

    for h in range(halves):
        for i in pairs:
            first(h, i).wait_recv()
        out_ref[blk, h, grp] = spread[h][source[grp]]
        for i in pairs:
            a = partner(i)
            arranged[h, a] = spread[h][source[a]]
            second(h, i).start()
            if h > 0:
                forward(h - 1, i)
        forward(h, 0)
    for i in pairs:
        forward(halves - 1, i)

    copy_p.wait()
    accumulate(blk, blocks == 1)

    for k in range(1, blocks):
        for h in range(halves):
            for i in [0] + pairs:
                third(h, i, k).wait_recv()

        accumulate(lax.rem(blk + blocks - k, blocks), k == blocks - 1)

    for h in range(halves):
        for i in [0] + pairs:
            for k in range(1, blocks):
                third(h, i, k).wait_send()

        for i in pairs:
            first(h, i).wait_send()
            second(h, i).wait_send()

    for j in range(slots):
        pltpu.make_async_copy(total_v.at[j], out_hbm.at[j], out_sems.at[j]).wait()


def shards(
    walker_matrix,
    updates,
    update_rows,
    left_table,
    right_table,
    assignment,
    momentum_sum,
    transfer_momentum,
    transfer_frequency,
    ownership,
    g4_prior,
):
    groups = lax.axis_size("grp")
    blocks = lax.axis_size("blk")
    order, kw = left_table.shape
    number, rank = updates.shape[2], updates.shape[4]
    smem = pl.BlockSpec(memory_space=pltpu.SMEM)
    hbm = pl.BlockSpec(memory_space=pltpu.HBM)
    halves = 2 if kw // groups % 16 == 0 else 1
    rows = kw // groups // halves
    slots = g4_prior.shape[1]
    summed = pl.pallas_call(
        functools.partial(exchange_kernel, groups, blocks),
        out_shape=jax.ShapeDtypeStruct((slots, kw, kw), F32),
        in_specs=[smem] * 5 + [hbm] * 6,
        out_specs=hbm,
        scratch_shapes=[
            pltpu.VMEM((order, order), F32),
            pltpu.VMEM((number, order, rank), BF16),
            pltpu.VMEM((number, rank), jnp.int32),
            pltpu.VMEM((order, kw), F32),
            pltpu.VMEM((order, kw), F32),
            pltpu.VMEM((number, order, rank), BF16),
            pltpu.VMEM((order, kw), BF16),
            pltpu.VMEM((order, kw), BF16),
            pltpu.VMEM((halves, groups, rows, kw), F32),
            pltpu.VMEM((halves, groups, rows, kw), F32),
            pltpu.VMEM((blocks, halves, groups, rows, kw), F32),
            pltpu.VMEM((slots * kw, kw), BF16),
            pltpu.VMEM((slots, kw, kw), F32),
            pltpu.SMEM((groups,), jnp.int32),
            pltpu.SemaphoreType.DMA((number + 8,)),
            pltpu.SemaphoreType.DMA((slots,)),
            pltpu.SemaphoreType.DMA((halves, groups)),
            pltpu.SemaphoreType.DMA((halves, groups)),
            pltpu.SemaphoreType.DMA((halves, groups)),
            pltpu.SemaphoreType.DMA((halves, groups)),
            pltpu.SemaphoreType.DMA((halves, groups, blocks)),
            pltpu.SemaphoreType.DMA((halves, groups, blocks)),
        ] + [pltpu.VMEM((groups, rows, kw), F32)] * halves,
        compiler_params=pltpu.CompilerParams(
            collective_id=0, has_side_effects=True, vmem_limit_bytes=63 * 2**20 + 2**19),
        name="exchange",
    )(assignment, ownership, transfer_momentum, transfer_frequency, momentum_sum,
      walker_matrix[0, 0], updates[0, 0], update_rows[0, 0], left_table, right_table, g4_prior[0])
    return summed[None]


def solution(mesh):
    placed = (
        P("grp", "blk", None, None),
        P("grp", "blk", None, None, None),
        P("grp", "blk", None, None),
        P(),
        P(),
        P("blk", None),
        P(),
        P(),
        P(),
        P("blk"),
        P("grp", "blk", None, None),
    )
    return jax.shard_map(
        shards, mesh=mesh, in_specs=placed, out_specs=P("grp", "blk", None, None), check_vma=False
    )
```
